32 devices in a mesh: row: 8 (over z, y), col: 4 (over x, core).
Axes of the slice: x: 2, y: 2, z: 4, core: 2. Of those that a mesh axis runs over, the one named last changes fastest.
Arguments:
- queries: bfloat16 [1024, 1024], P('row', 'col'), may hold values from -26 to 26
- key_vectors: bfloat16 [1024, 1024], P('row', 'col'), may hold values from -8 to 8
- values: bfloat16 [1024, 1024], P('row', 'col'), may hold values from -6 to 6
- sink_logit: float32 [8], P('col'), may hold values from -1 to 5
- lengths: int32 [8], replicated, may hold values from 1 to 576, as said below
- stream: bfloat16 [1024, 2048], P('row', 'col'), may hold values from -60 to 60
- out_weight: bfloat16 [1024, 2048], P('col', 'row'), may hold values from -0.1875 to 0.1875
- norm_gain: bfloat16 [2048], P('col'), may hold values from 0.25 to 1.75
- shared_gate: bfloat16 [2048, 2816], P('row', 'col'), may hold values from -0.125 to 0.125
- shared_up: bfloat16 [2048, 2816], P('row', 'col'), may hold values from -0.125 to 0.125
- shared_down: bfloat16 [2816, 2048], P('col', 'row'), may hold values from -0.109375 to 0.109375
- shared_switch: bfloat16 [2048], replicated, may hold values from -0.125 to 0.125
- expert_gate: bfloat16 [8, 2048, 1408], P('row', None, 'col'), may hold values from -0.125 to 0.125
- expert_up: bfloat16 [8, 2048, 1408], P('row', None, 'col'), may hold values from -0.125 to 0.125
- expert_down: bfloat16 [8, 1408, 2048], P('row', 'col'), may hold values from -0.15625 to 0.15625
- routes: int32 [1024, 4], P('row'), may hold values from 0 to 7, all different within a row; in each aligned block of 128 rows (0 to 127, 128 to 255, ...) at most 96 rows name the same one
- route_weights: float32 [1024, 4], P('row'), may hold values from 0.05 to 0.6
Outputs:
- attended: bfloat16 [1024, 1024], P('row', 'col')
- layer_out: bfloat16 [1024, 2048], P('row', 'col')
The draws below stay inside these ranges and needn't reach their ends.
Inputs may be any that keep to these rules, and one draw needn't show every extreme that they name: `routes`: each row names 4 different experts; among the 128 rows of one device (aligned blocks) no expert is named more than 96 times, a bound that some block reaches. The lengths sum to 1024; exactly one prompt has 576 tokens.
All inputs are finite; a program needn't handle non-finite values.
Results may differ from the reference program's by a relative error of at most 0.01.
Values may be sent and summed in bfloat16 or wider, within the bound.
A program may use at most 128 MiB of HBM per device.

```python
import math
import jax
import jax.numpy as jnp
import numpy as np
from jax import lax

D = 2048
FFE = 1408
HEADS = 8
HDIM = 128
SHARED = 2816
TOP = 4
WINDOW = 4096
TOK_DEV = 128
TOKENS = 1024
EXPERTS = 8
LONGEST = 576
DOCS = 8
CAP = 96
N_ROW = 8
N_COL = 4


def draw_lengths(key, part):
    cut_key = jax.random.fold_in(key, 41)
    place_key = jax.random.fold_in(key, 42)
    remaining = TOKENS - LONGEST
    shuffled = jax.random.permutation(cut_key, remaining - 1) + 1
    cuts = jnp.sort(shuffled[:DOCS - 2]).astype(jnp.int32)
    bounds = jnp.concatenate([jnp.zeros((1,), jnp.int32), cuts, jnp.full((1,), remaining, jnp.int32)])
    pieces = (bounds[1:] - bounds[:-1]).astype(jnp.int32)
    where_long = jax.random.randint(place_key, (), 0, DOCS)
    slots = jnp.arange(DOCS, dtype=jnp.int32)
    earlier = pieces[jnp.minimum(slots, DOCS - 2)]
    later = pieces[jnp.maximum(slots - 1, 0)]
    result = jnp.where(slots < where_long, earlier, jnp.where(slots == where_long, LONGEST, later))
    return result.astype(jnp.int32)


def key_table(key):
    inner_key = jax.random.fold_in(key, 21)
    raw_keys = jnp.clip(2.0 * jax.random.normal(inner_key, (TOKENS, HEADS * HDIM)), -8.0, 8.0)
    return raw_keys


def draw_key_vectors(key, part):
    return key_table(key).astype(jnp.bfloat16)


def draw_queries(key, part):
    inner_key = jax.random.fold_in(key, 22)
    raw_queries = jnp.clip(jax.random.normal(inner_key, (TOKENS, HEADS * HDIM)), -4.0, 4.0)
    return raw_queries.astype(jnp.bfloat16)


def draw_stream(key, part):
    noise_key = jax.random.fold_in(key, 31)
    line_key = jax.random.fold_in(key, 32)
    column_key = jax.random.fold_in(key, 33)
    line_scale = jnp.exp(jax.random.uniform(line_key, (TOKENS, 1), minval=math.log(0.3), maxval=math.log(3.0)))
    column_rough = jnp.exp(jax.random.uniform(column_key, (1, D), minval=math.log(0.5), maxval=math.log(2.0)))
    column_place = (jnp.arange(D, dtype=jnp.float32) / D)[None, :]
    column_scale = column_rough * 0.4 * jnp.exp(math.log(6.0) * column_place)
    noise = jnp.clip(jax.random.normal(noise_key, (TOKENS, D)), -4.0, 4.0)
    result = noise * line_scale * column_scale
    return result.astype(jnp.bfloat16)


def shard_levels(rng, dims, cuts, low, top_value):
    def one(position, shards_of):
        draws = jax.random.uniform(jax.random.fold_in(jax.random.fold_in(rng, 6), position), (shards_of,), jnp.float32, low / len(cuts), top_value / len(cuts))
        return jnp.repeat(jnp.exp(draws), dims[position] // shards_of).reshape((-1,) + (1,) * (len(dims) - position - 1))

    level = one(*cuts[0])
    for cut in cuts[1:]:
        level = level * one(*cut)
    return level


def routed_block(stream_key, own, number, rows, count, top, limit, slope):
    ranking = jax.random.permutation(stream_key, count)
    crowded, usual = load_shares(count, rows * top, limit, slope, True), load_shares(count, rows * top, limit, slope, False)
    places = jnp.arange(count)

    def named(sizes, turn):
        used = int((sizes > 0).sum())
        fixed = max(1, used // 4)
        moved = fixed + (places - fixed + turn * (used - fixed)) % max(1, count - fixed)
        return jnp.zeros((count,), jnp.int32).at[ranking[jnp.where(places < fixed, places, moved)]].set(jnp.asarray(sizes, jnp.int32))

    sizes = jnp.where(number % 4 == 0, named(crowded, number // 4), named(usual, number - number // 4 - 1))
    mixed = jax.random.permutation(jax.random.fold_in(own, 3), count)
    donor, receiver = mixed[0:count // 2 * 2:2], mixed[1:count // 2 * 2:2]
    slack = jnp.minimum(sizes[donor] - 1, limit - sizes[receiver]) // 2
    slack = jnp.where((donor == ranking[0]) | (receiver == ranking[0]) | (sizes[receiver] == 0), 0, jnp.maximum(slack, 0))
    moved = jax.random.randint(jax.random.fold_in(own, 4), (count // 2,), 0, 1 << 20) % (slack + 1)
    sizes = sizes.at[donor].add(-moved).at[receiver].add(moved)
    members = jnp.searchsorted(jnp.cumsum(sizes), jnp.arange(rows * top), side="right").astype(jnp.int32)
    grid = members.reshape(top, rows).T
    grid = grid[jax.random.permutation(jax.random.fold_in(own, 1), rows)]
    turn = jax.random.randint(jax.random.fold_in(own, 2), (rows, 1), 0, top)
    return jnp.take_along_axis(grid, (jnp.arange(top)[None, :] + turn) % top, axis=1)


def load_shares(number_of, total, bound, skew, full):
    portions = [(1 << 20) // math.isqrt(standing ** skew) + 1 for standing in range(1, number_of + 1)]
    largest = bound if full else min(bound, max(-(-total // number_of), total * portions[0] // sum(portions)))
    least = 1 if total - largest >= number_of - 1 else 0
    given, spare = [largest] + [least] * (number_of - 1), total - largest - least * (number_of - 1)
    while spare > 0:
        free = [i for i in range(1, number_of) if given[i] < largest] or [i for i in range(1, number_of) if given[i] < bound]
        pool, left = sum([portions[i] for i in free]), spare
        for i in free:
            addition = min(bound - given[i], max(1, left * portions[i] // pool), spare)
            given[i] = given[i] + addition
            spare = spare - addition
    return np.array(given)


def normal_values(stream_key, shape, scale, reach, split=(), held_as=jnp.bfloat16):
    level = shard_levels(stream_key, shape, split, -0.22, 0.18) if split else 1.0
    drawn = jax.random.normal(stream_key, shape, jnp.float32) * scale * level
    return jnp.minimum(jnp.maximum(drawn, -reach), reach).astype(held_as)


def setup_inputs(seed: int = 0) -> dict:
    seeds = jax.random.split(jax.random.key(seed), 18)
    queries = draw_queries(jax.random.fold_in(seeds[17], 71), 0)
    key_vectors = draw_key_vectors(jax.random.fold_in(seeds[17], 71), 0)
    values = normal_values(seeds[2], (TOKENS, HEADS * HDIM), 1.0, 6.0, ((0, 8), (1, 4)))
    sink_logit = jnp.clip(-1.0 + 6.0 * jax.random.uniform(seeds[3], (HEADS,), jnp.float32) ** shard_levels(seeds[3], (HEADS,), ((0, 4),), -0.2, 0.2), -1.0, 5.0)
    lengths = draw_lengths(jax.random.fold_in(seeds[17], 71), 0)
    stream = draw_stream(jax.random.fold_in(seeds[17], 71), 0)
    out_weight = normal_values(seeds[6], (HEADS * HDIM, D), (HEADS * HDIM) ** -0.5, 0.1875, ((0, 4), (1, 8)))
    norm_gain = jnp.clip(1.0 + 0.15 * jax.random.normal(seeds[7], (D,), jnp.float32), 0.25, 1.75).astype(jnp.bfloat16)
    shared_gate = normal_values(seeds[8], (D, SHARED), D ** -0.5, 0.125, ((0, 8), (1, 4)))
    shared_up = normal_values(seeds[9], (D, SHARED), D ** -0.5, 0.125, ((0, 8), (1, 4)))
    shared_down = normal_values(seeds[10], (SHARED, D), SHARED ** -0.5, 0.109375, ((0, 4), (1, 8)))
    shared_switch = normal_values(seeds[11], (D,), D ** -0.5, 0.125)
    expert_gate = normal_values(seeds[12], (EXPERTS, D, FFE), D ** -0.5, 0.125, ((0, 8), (2, 4)))
    expert_up = normal_values(seeds[13], (EXPERTS, D, FFE), D ** -0.5, 0.125, ((0, 8), (2, 4)))
    expert_down = normal_values(seeds[14], (EXPERTS, FFE, D), FFE ** -0.5, 0.15625, ((0, 8), (1, 4)))
    routes_keys = jax.random.split(jax.random.fold_in(seeds[15], 1), TOKENS // TOK_DEV)
    routes_turns = jax.random.permutation(jax.random.fold_in(seeds[15], 3), TOKENS // TOK_DEV)
    routes = jax.vmap(lambda own, number: routed_block(jax.random.fold_in(seeds[15], 2), own, number, TOK_DEV, EXPERTS, TOP, CAP, 2))(routes_keys, routes_turns).reshape((TOKENS, TOP))
    route_weights = jnp.clip(jnp.exp(math.log(0.6) - 2.4849067 * jax.random.uniform(seeds[16], (TOKENS, TOP), jnp.float32) ** shard_levels(seeds[16], (TOKENS, TOP), ((0, 8),), -0.2, 0.2)), 0.05, 0.6)
    return {"queries": queries, "key_vectors": key_vectors, "values": values, "sink_logit": sink_logit, "lengths": lengths, "stream": stream, "out_weight": out_weight, "norm_gain": norm_gain, "shared_gate": shared_gate, "shared_up": shared_up, "shared_down": shared_down, "shared_switch": shared_switch, "expert_gate": expert_gate, "expert_up": expert_up, "expert_down": expert_down, "routes": routes, "route_weights": route_weights}


norm_eps = 1e-06
masked_score = -1e+30

def lower_bounds(lengths, positions):
    doc_ends = jnp.cumsum(lengths).astype(jnp.int32)
    starts = (doc_ends - lengths).astype(jnp.int32)
    begun_docs = starts[None, :] <= positions[:, None]
    doc_start = lax.optimization_barrier(jnp.max(jnp.where(begun_docs, starts[None, :], 0), axis=1)).astype(jnp.int32)
    return jnp.maximum(doc_start, positions - WINDOW + 1).astype(jnp.int32)

def attend(queries, key_vectors, values, sink_logit, lower_bound):
    span = min(512, TOKENS)
    score_scale = 1.0 / math.sqrt(HDIM)
    key_heads = key_vectors.reshape(TOKENS, HEADS, HDIM).astype(jnp.float32)
    value_heads = values.reshape(TOKENS, HEADS, HDIM).astype(jnp.float32)
    key_places = jnp.arange(TOKENS, dtype=jnp.int32)

    def one_block(block_index):
        first_row = block_index * span
        query_block = lax.dynamic_slice_in_dim(queries, first_row, span, 0).reshape(span, HEADS, HDIM).astype(jnp.float32)
        low_bound = lax.dynamic_slice_in_dim(lower_bound, first_row, span, 0)
        positions = first_row + jnp.arange(span, dtype=jnp.int32)
        scores = jnp.einsum('qhd,khd->hqk', query_block, key_heads) * score_scale
        visible = ((key_places[None, :] >= low_bound[:, None]) & (key_places[None, :] <= positions[:, None]))[None]
        masked = jnp.where(visible, scores, masked_score)
        row_max = jnp.maximum(lax.optimization_barrier(jnp.max(masked, axis=2)), sink_logit[:, None])
        weight = jnp.where(visible, jnp.exp(masked - row_max[:, :, None]), 0.0)
        denominator = lax.optimization_barrier(jnp.sum(weight, axis=2)) + jnp.exp(sink_logit[:, None] - row_max)
        rounded = lax.optimization_barrier(weight.astype(jnp.bfloat16)).astype(jnp.float32)
        mixture = jnp.einsum('hqk,khd->hqd', rounded, value_heads) / denominator[:, :, None]
        return jnp.transpose(mixture, (1, 0, 2)).reshape(span, HEADS * HDIM).astype(jnp.bfloat16)
    blocks = lax.map(one_block, jnp.arange(TOKENS // span, dtype=jnp.int32))
    return blocks.reshape(TOKENS, HEADS * HDIM)

def expert_table(routes):
    flat_routes = routes.reshape(N_ROW, TOK_DEV * TOP)
    onehot = (flat_routes[:, :, None] == jnp.arange(EXPERTS, dtype=jnp.int32)[None, None, :]).astype(jnp.int32)
    before = (jnp.cumsum(onehot, axis=1) - onehot).astype(jnp.int32)
    slot_index = lax.optimization_barrier(jnp.sum(before * onehot, axis=2)).astype(jnp.int32)
    device_block = jnp.arange(N_ROW, dtype=jnp.int32)[:, None]
    target = (flat_routes * (N_ROW * CAP) + device_block * CAP + slot_index).reshape(-1).astype(jnp.int32)
    owner_row = (jnp.arange(TOKENS * TOP, dtype=jnp.int32) // TOP).astype(jnp.int32)
    source = jnp.full((EXPERTS * N_ROW * CAP,), TOKENS, jnp.int32).at[target].set(owner_row)
    return (target, source)

def experts_apply(normed, routes, route_weights, expert_gate, expert_up, expert_down):
    target, source = expert_table(routes)
    slot_weight = jnp.zeros((EXPERTS * N_ROW * CAP,), jnp.float32).at[target].set(route_weights.reshape(-1))
    padded = jnp.concatenate([normed, jnp.zeros((1, D), jnp.bfloat16)], 0)
    source = source.reshape(EXPERTS, N_ROW * CAP)
    slot_weight = slot_weight.reshape(EXPERTS, N_ROW * CAP)
    group = FFE // N_COL

    def per_expert(accum, expert_index):
        picked = source[expert_index]
        dispatched = padded[picked]
        gate_out = jnp.dot(dispatched, expert_gate[expert_index], preferred_element_type=jnp.float32)
        up_out = jnp.dot(dispatched, expert_up[expert_index], preferred_element_type=jnp.float32)
        activation = (jax.nn.silu(gate_out) * up_out).astype(jnp.bfloat16)
        partials = jnp.einsum('mcf,cfd->cmd', activation.reshape(-1, N_COL, group).astype(jnp.float32), expert_down[expert_index].reshape(N_COL, group, D).astype(jnp.float32))
        part_sum = lax.optimization_barrier(jnp.sum(lax.optimization_barrier(partials.astype(jnp.bfloat16)).astype(jnp.float32), axis=0))
        accum = accum.at[picked].add(slot_weight[expert_index][:, None] * part_sum)
        return (accum, None)
    accum, unused = lax.scan(per_expert, jnp.zeros((TOKENS + 1, D), jnp.float32), jnp.arange(EXPERTS, dtype=jnp.int32))
    return accum[:TOKENS]

def reference(queries, key_vectors, values, sink_logit, lengths, stream, out_weight, norm_gain, shared_gate, shared_up, shared_down, shared_switch, expert_gate, expert_up, expert_down, routes, route_weights):
    positions = jnp.arange(TOKENS, dtype=jnp.int32)
    lower_bound = lower_bounds(lengths, positions)
    attended = attend(queries, key_vectors, values, sink_logit, lower_bound)
    hidden = (stream.astype(jnp.float32) + jnp.dot(attended, out_weight, preferred_element_type=jnp.float32)).astype(jnp.bfloat16)
    widened = hidden.astype(jnp.float32)
    normed = (widened * lax.rsqrt(lax.optimization_barrier(jnp.mean(widened * widened, axis=1, keepdims=True)) + norm_eps) * norm_gain.astype(jnp.float32)).astype(jnp.bfloat16)
    shared_gate_out = jnp.dot(normed, shared_gate, preferred_element_type=jnp.float32)
    shared_up_out = jnp.dot(normed, shared_up, preferred_element_type=jnp.float32)
    shared_act = (jax.nn.silu(shared_gate_out) * shared_up_out).astype(jnp.bfloat16)
    shared_out = jnp.dot(shared_act, shared_down, preferred_element_type=jnp.float32)
    switch = jax.nn.sigmoid(jnp.dot(normed, shared_switch, preferred_element_type=jnp.float32))
    routed = experts_apply(normed, routes, route_weights, expert_gate, expert_up, expert_down)
    layer_out = (widened + switch[:, None] * shared_out + routed).astype(jnp.bfloat16)
    return (attended, layer_out)
```

```python
import math

import jax
import jax.numpy as jnp
from jax import lax
from jax.experimental import pallas as pl
from jax.experimental.pallas import tpu as pltpu
from jax.sharding import PartitionSpec as P

HDIM = 128
WINDOW = 4096


norm_eps = 1e-06
masked_score = -1e30


def lower_bounds(lengths, positions):
    order = jnp.arange(lengths.shape[0])
    earlier = order[None, :] < order[:, None]
    starts = jnp.sum(jnp.where(earlier, lengths[None, :], 0), axis=1)
    begun_docs = starts[None, :] <= positions[:, None]
    doc_start = jnp.max(jnp.where(begun_docs, starts[None, :], 0), axis=1)
    return jnp.maximum(doc_start, positions - WINDOW + 1)


MESH = pl.DeviceIdType.MESH
LONGEST = 576
ROWS = 8
COLS = 4
TOK = 128
WIDTH = 2048
PART = WIDTH // COLS
SLICE = WIDTH // ROWS
UNITS = 96
REACH = (LONGEST - 2 + TOK) // TOK
HOPS = REACH // 2
DEPTH = ROWS // 2
PLANE = 2 * TOK
CHUNKS = 2
PIECE = TOK // CHUNKS
STEPS = DEPTH * CHUNKS
NT = (((1,), (1,)), ((), ()))


def mm(a, b):
    return jnp.dot(a, b, preferred_element_type=jnp.float32)


def layer_kernel(
    q_hbm,
    k_hbm,
    v_hbm,
    sink_hbm,
    lengths_hbm,
    stream_hbm,
    wo_hbm,
    gain_hbm,
    sg_hbm,
    su_hbm,
    sd_hbm,
    switch_hbm,
    eg_hbm,
    eu_hbm,
    ed_hbm,
    routes_hbm,
    route_weights_hbm,
    att_ref,
    out_ref,
    q_ref,
    sink_ref,
    lengths_ref,
    gain_ref,
    switch_ref,
    routes_ref,
    route_weights_ref,
    weights,
    gain_send,
    switch_buf,
    w_send,
    kv_buf,
    wo_buf,
    gain_buf,
    w_buf,
    share_buf,
    att_all,
    stream_all,
    head_send,
    head_recv,
    cross_send,
    cross_recv,
    hid,
    keep,
    send1,
    recv1,
    send2,
    recv2,
    send3,
    recv3,
    send4,
    recv4,
    s_local,
    s_kv,
    r_kv,
    s_wo,
    r_wo,
    s_gain,
    r_gain,
    s_sh,
    r_sh,
    s_w,
    r_w,
    s_pair,
    r_pair,
    s_head,
    r_head,
    s_z,
    r_z,
    s_a,
    r_a,
    s_b,
    r_b,
    s_c,
    r_c,
    s_1,
    r_1,
    s_2,
    r_2,
    s_3,
    r_3,
    s_4,
    r_4,
):
    r = lax.axis_index("row")
    c = lax.axis_index("col")
    z = r // 2
    y = r % 2
    x = c // 2
    core = c % 2
    partner = r + 1 - 2 * y
    core_peer = c + 1 - 2 * core
    x_peer = (c + 2) % COLS
    peer_a = (r + (1 - core) * (partner - r), c + core * (x_peer - c))
    peer_b = (r + core * (partner - r), c + (1 - core) * (x_peer - c))

    def ahead(d):
        return ((z + d) % DEPTH) * 2 + y

    def behind(d):
        return (z + DEPTH - d) % DEPTH

    high = z // 2
    outer = ((z + 1) // 2 + 1) % 2
    edge = 3 * high * 2 + y

    def turn(j):
        near_first = outer * j + (1 - outer) * (j + (j // 2) * (5 - 2 * j))
        return (high * near_first + (1 - high) * (DEPTH - near_first)) % DEPTH

    def straight(d):
        return (z < DEPTH - 1, outer == 1, z > 0)[d - 1]

    def up(k):
        return (r + k) % ROWS

    def down(k):
        return (r + ROWS - k) % ROWS

    def cols(i, n):
        return pl.ds(pl.multiple_of(i * n, n), n)

    def spot(a, b, lane):
        return (x + b * (1 - lane) + a * lane) % 2, (y + a * (1 - lane) + b * lane) % 2

    routed_units = eg_hbm.shape[0]
    shared_hbm = (sg_hbm, su_hbm, sd_hbm)

    def sh_src(i, row):
        first = (row // 2) * 176 + (row % 2) * 80
        return shared_hbm[i].at[pl.ds(pl.multiple_of(first, 16), UNITS)]

    def sh_dst(i, row):
        return weights.at[i, routed_units : routed_units + UNITS, cols(row, SLICE)]

    early = (
        (k_hbm, kv_buf.at[0, 0:TOK]),
        (v_hbm, kv_buf.at[1, 0:TOK]),
        (q_hbm, q_ref),
        (gain_hbm, gain_ref),
        (routes_hbm, routes_ref),
        (route_weights_hbm, route_weights_ref),
        (lengths_hbm, lengths_ref),
        (sink_hbm, sink_ref),
        (switch_hbm, switch_ref),
        (wo_hbm, wo_buf.at[:, cols(z, SLICE)]),
        (stream_hbm.at[:, cols(y, SLICE)], stream_all.at[cols(y, TOK)]),
    )
    late = tuple(
        (a, weights.at[i, 0:routed_units]) for i, a in enumerate((eg_hbm, eu_hbm, ed_hbm))
    ) + tuple((sh_src(i, r), sh_dst(i, r)) for i in range(3))
    locals_ = [
        pltpu.make_async_copy(a, b, s_local.at[i]) for i, (a, b) in enumerate(early + late)
    ]

    barrier = pltpu.get_barrier_semaphore()
    for k in range(1, ROWS):
        pl.semaphore_signal(barrier, inc=1, device_id=(up(k), c), device_id_type=MESH)
    for k in range(1, COLS):
        pl.semaphore_signal(barrier, inc=1, device_id=(r, (c + k) % COLS), device_id_type=MESH)
    for copy in locals_:
        copy.start()
    pl.semaphore_wait(barrier, ROWS - 1 + COLS - 1)

    def push(src, dst, send, recv, where):
        return pltpu.make_async_remote_copy(
            src_ref=src,
            dst_ref=dst,
            send_sem=send,
            recv_sem=recv,
            device_id=where,
            device_id_type=MESH,
        )

    def kv_copy(i, from_slot, to_slot, sem, row):
        own = (k_hbm, v_hbm)[i]
        src = own if from_slot == 0 else kv_buf.at[i, pl.ds(from_slot * TOK, TOK)]
        dst = kv_buf.at[i, cols(to_slot, TOK)]
        return push(src, dst, s_kv.at[i, sem], r_kv.at[i, to_slot], (row, c))

    def wo_copy(d, at):
        return push(wo_hbm, wo_buf.at[:, cols(at, SLICE)], s_wo.at[d], r_wo.at[d], (ahead(d), c))

    def wo_relay(i):
        d = high * i + (1 - high) * (DEPTH - i)
        block = wo_buf.at[:, cols(behind(d), SLICE)]
        arrival = push(block, block, s_wo.at[0], r_wo.at[d], (edge, c))
        onward = push(block, block, s_wo.at[DEPTH - 1 + i], r_wo.at[d + 2 * high - 1], (edge, c))
        return arrival, onward

    def sh_copy(i, k, row):
        sem = i * ROWS + k
        return push(sh_src(i, up(k)), sh_dst(i, row), s_sh.at[sem], r_sh.at[sem], (up(k), c))

    def w_copy(k):
        return push(w_send.at[up(k)], w_buf.at[k], s_w.at[k], r_w.at[k], (up(k), c))

    def gain_copy(k, block):
        return push(
            gain_send,
            gain_buf.at[:, cols(block, PART)],
            s_gain.at[k],
            r_gain.at[k],
            (r, (c + k) % COLS),
        )

    def stream_copy(at):
        src = stream_hbm.at[:, cols(1 - y, SLICE)]
        return push(src, stream_all.at[cols(at, TOK)], s_pair.at[0], r_pair.at[0], (partner, c))

    def att_copy(at):
        return push(att_ref, att_all.at[cols(at, TOK)], s_pair.at[1], r_pair.at[1], (partner, c))

    def head_copy(i):
        return push(head_send.at[i], head_recv.at[i], s_head.at[i], r_head.at[i], (r, core_peer))

    def cross_copy():
        return push(cross_send, cross_recv, s_head.at[2], r_head.at[2], (r, x_peer))

    def both(fn, *args):
        for i in range(2):
            getattr(kv_copy(i, *args), fn)()

    near = 2 * HOPS

    def sends(fn):
        for d in range(1, HOPS + 1):

            @pl.when(z + d < DEPTH)
            def _():
                both(fn, 0, 2 * d, d, jnp.minimum(r + 2 * d, ROWS - 1))

        @pl.when(y == 0)
        def _():
            both(fn, 0, 1, 0, partner)

        @pl.when(r == 1)
        def _():
            both(fn, 0, REACH, near + 1, r + REACH)

    def handovers(fn):
        for d in range(1, HOPS + 1):

            @pl.when(z >= d)
            def _():
                for i in range(2):
                    if fn == "relay":
                        kv_copy(i, 0, 2 * d, 0, partner).wait_recv()
                    onward = kv_copy(i, 2 * d, 2 * d + 1 - 2 * y, HOPS + d, partner)
                    getattr(onward, "start" if fn == "relay" else fn)()

    def arrived(k):
        @pl.when(r >= k)
        def _():
            both("wait_recv", 0, k, 0, partner)

    def wo_sends(fn):
        for d in (1, 3, 2):

            @pl.when(straight(d))
            def _():
                getattr(wo_copy(d, z), fn)()

    sends("start")
    wo_sends("start")
    stream_copy(y).start()

    for copy in locals_[: len(early)]:
        copy.wait()
    for i in range(PART // HDIM):
        gain_send[:, i * HDIM : (i + 1) * HDIM] = jnp.broadcast_to(
            gain_ref[i : i + 1, :].astype(jnp.float32), (8, HDIM)
        )
    for e in range(ROWS):
        picked = jnp.where(routes_ref[...] == e, route_weights_ref[...], 0.0)
        w_send[e] = jnp.broadcast_to(jnp.sum(picked, axis=0, keepdims=True), (8, TOK))
    for k in range(1, COLS):
        gain_copy(k, c).start()
    for k in range(1, ROWS):
        w_copy(k).start()

    gain_buf[:, cols(c, PART)] = gain_send[...]
    w_buf[0] = w_send[r]
    for i in range(WIDTH // HDIM):
        switch_buf[:, i * HDIM : (i + 1) * HDIM] = jnp.broadcast_to(
            switch_ref[i : i + 1, :].astype(jnp.float32), (8, HDIM)
        )

    for k in range(1, REACH + 1):

        @pl.when(r < k)
        def _():
            kv_buf[:, k * TOK : (k + 1) * TOK] = jnp.zeros((2, TOK, 2 * HDIM), jnp.bfloat16)

    handovers("relay")

    @pl.when(outer == 0)
    def _():
        for i in range(1, 3):
            arrival, onward = wo_relay(i)
            arrival.wait_recv()
            onward.start()

    for k in range(1, REACH + 1, 2):
        arrived(k)

    keys = (REACH + 1) * TOK
    place = lax.broadcasted_iota(jnp.int32, (TOK, keys), 1)
    key_place = (r - place // TOK) * TOK + place % TOK
    rows_at = r * TOK + lax.broadcasted_iota(jnp.int32, (TOK, 1), 0)
    lower = jnp.maximum(rows_at - WINDOW + 1, 0)
    begin = jnp.int32(0)
    for d in range(lengths_ref.shape[0]):
        lower = jnp.maximum(lower, jnp.where(rows_at >= begin, begin, 0))
        begin = begin + lengths_ref[d]
    visible = (key_place >= lower) & (key_place <= rows_at)
    for h in range(2):
        lanes = slice(h * HDIM, (h + 1) * HDIM)
        scores = lax.dot_general(
            q_ref[:, lanes], kv_buf[0, :, lanes], NT, preferred_element_type=jnp.float32
        ) * (1.0 / math.sqrt(HDIM))
        masked = jnp.where(visible, scores, masked_score)
        sink = sink_ref[h]
        row_max = jnp.maximum(jnp.max(masked, axis=1, keepdims=True), sink)
        weight = jnp.where(visible, jnp.exp(masked - row_max), 0.0)
        denominator = jnp.exp(sink - row_max) + jnp.sum(weight, axis=1, keepdims=True)
        mixture = mm(weight.astype(jnp.bfloat16), kv_buf[1, :, lanes])
        att_ref[:, lanes] = (mixture / denominator).astype(jnp.bfloat16)

    att_copy(y).start()
    att_all[cols(y, TOK)] = att_ref[...]
    for d in range(1, DEPTH):
        already = (z == 2, outer == 0, z == 1)[d - 1]

        @pl.when(jnp.logical_not(already))
        def _():
            wo_copy(d, behind(d)).wait_recv()

    for k in range(1, ROWS):
        for i in range(3):
            sh_copy(i, k, r).start()

    att_copy(1 - y).wait_recv()
    attended = att_all[...]

    def term(side, lane):
        return mm(attended, wo_buf[:, cols(2 * side + lane, SLICE)])

    head_send[0] = term(1 - x, 1 - core).astype(jnp.bfloat16)
    head_copy(0).start()
    head_send[1] = term(x, 1 - core).astype(jnp.bfloat16)
    head_copy(1).start()
    far = term(1 - x, core)
    stream_copy(1 - y).wait_recv()
    total = stream_all[...].astype(jnp.float32) + term(x, core)
    head_copy(0).wait_recv()
    cross_send[...] = (far + head_recv[0].astype(jnp.float32)).astype(jnp.bfloat16)
    cross_copy().start()
    head_copy(1).wait_recv()
    total = total + head_recv[1].astype(jnp.float32)
    cross_copy().wait_recv()
    total = total + cross_recv[...].astype(jnp.float32)

    def piece(d, a, b, lane):
        side, half = spot(a, b, lane)
        return hid.at[cols(behind(d), PLANE), cols(2 * (2 * side + lane) + half, SLICE)]

    hid[cols(z, PLANE), cols(2 * c + y, SLICE)] = total.astype(jnp.bfloat16)

    def z_copy(d, at):
        block = piece(at, 0, 0, core)
        return push(block, block, s_z.at[d], r_z.at[d], (ahead(d), c))

    def a_copy(d, a):
        block = piece(d, a, 0, core)
        return push(block, block, s_a.at[d], r_a.at[d], peer_a)

    def b_copy(d, a, b):
        block = piece(d, a, b, core)
        return push(block, block, s_b.at[2 * d + a], r_b.at[2 * d + a], peer_b)

    def c_copy(d, a, b, lane):
        block = piece(d, a, b, lane)
        sem = 4 * d + 2 * a + b
        return push(block, block, s_c.at[sem], r_c.at[sem], (r, core_peer))

    def z_relay(j):
        d = turn(j)
        block = piece(d, 0, 0, core)
        return push(block, block, s_z.at[DEPTH - 1 + j], r_z.at[d + 2 * high - 1], (edge, c))

    def z_sends(fn):
        for d in (1, 3, 2):

            @pl.when(straight(d))
            def _():
                getattr(z_copy(d, 0), fn)()

    z_sends("start")

    def spread(j):
        d = turn(j)
        if j > 0:
            z_copy(d, d).wait_recv()
        if j in (1, 3):

            @pl.when(outer == 0)
            def _():
                z_relay(j).start()

        a_copy(d, 0).start()
        b_copy(d, 0, 0).start()
        c_copy(d, 0, 0, core).start()

    def relay(j):
        d = turn(j)
        a_copy(d, 1).wait_recv()
        b_copy(d, 1, 0).start()
        c_copy(d, 1, 0, core).start()

    def collect(j):
        d = turn(j)
        for a in range(2):
            b_copy(d, a, 1).wait_recv()
            c_copy(d, a, 1, core).start()

    spread(0)
    spread(1)
    relay(0)
    spread(2)
    relay(1)
    collect(1)
    spread(3)
    relay(2)
    collect(2)

    for k in range(1, ROWS):
        for i in range(3):
            sh_copy(i, k, down(k)).wait_recv()
        w_copy(k).wait_recv()
    for k in range(1, COLS):
        gain_copy(k, (c + COLS - k) % COLS).wait_recv()
    for copy in locals_[len(early) :]:
        copy.wait()
    for row in range(ROWS):
        line = w_buf[(r + ROWS - row) % ROWS, 0:1, :]
        share_buf[row] = jnp.broadcast_to(line, (TOK, TOK)).T

    def copy1(k, i):
        return push(send1.at[k, i], recv1.at[k, i], s_1.at[k, i], r_1.at[k, i], (r, core_peer))

    def copy2(k):
        return push(send2.at[k], recv2.at[k], s_2.at[k], r_2.at[k], peer_b)

    def copy3(k):
        return push(send3.at[k], recv3.at[k], s_3.at[k], r_3.at[k], peer_a)

    def copy4(k):
        return push(
            send4.at[k], recv4.at[k], s_4.at[k], r_4.at[k], (behind(k // CHUNKS) * 2 + y, c)
        )

    def block_of(s):
        return turn((s // CHUNKS + 1) % DEPTH) * CHUNKS + s % CHUNKS

    def experts(k):
        plane = behind(k // CHUNKS)
        part = k % CHUNKS
        rows = [
            pl.ds(pl.multiple_of((2 * plane + j) * TOK + part * PIECE, PIECE), PIECE)
            for j in range(2)
        ]
        widened = jnp.concatenate([hid[at, :] for at in rows], 0).astype(jnp.float32)
        mean = jnp.mean(widened * widened, axis=1, keepdims=True)
        normed = (widened * lax.rsqrt(mean + norm_eps) * gain_buf[0:1, :]).astype(jnp.bfloat16)
        logit = jnp.sum(normed.astype(jnp.float32) * switch_buf[0:1, :], axis=1, keepdims=True)
        switch = 1.0 / (1.0 + jnp.exp(-logit))
        share = jnp.concatenate(
            [share_buf[2 * plane + j, cols(part, PIECE), 0:1] for j in range(2)], 0
        )
        gate = lax.dot_general(normed, weights[0], NT, preferred_element_type=jnp.float32)
        raised = lax.dot_general(normed, weights[1], NT, preferred_element_type=jnp.float32)
        unit = lax.broadcasted_iota(jnp.int32, gate.shape, 1) - routed_units
        first = 16 * y
        last = first + UNITS - 16 + 16 * (1 - y)
        scale = jnp.where(unit < 0, share, jnp.where((unit >= first) & (unit < last), switch, 0.0))
        act = gate / (1.0 + jnp.exp(-gate)) * raised * scale
        act = act.astype(jnp.bfloat16)
        for i in range(2):
            out = mm(act, weights[2, :, cols(2 * i + 1 - core, PART)])
            send1[k, i] = out.astype(jnp.bfloat16).reshape(2, PIECE, PART)
            copy1(k, i).start()
        for i in range(2):
            out = mm(act, weights[2, :, cols(2 * i + core, PART)])
            keep[k, i] = out.reshape(2, PIECE, PART)

    def step(s, carry):
        @pl.when(s == 0)
        def _():
            relay(3)

        @pl.when(s == CHUNKS)
        def _():
            collect(3)
            collect(0)

        @pl.when((s < STEPS) & (s % CHUNKS == 0))
        def _():
            for a in range(2):
                for b in range(2):
                    c_copy(block_of(s) // CHUNKS, a, b, 1 - core).wait_recv()

        @pl.when(s < STEPS)
        def _():
            experts(block_of(s))

        @pl.when((s >= 1) & (s < STEPS + 1))
        def _():
            k = block_of(s - 1)
            for i in range(2):
                copy1(k, i).wait_recv()
                keep[k, i] = keep[k, i] + recv1[k, i].astype(jnp.float32)
            for a in range(2):
                side, half = spot(a, 1, core)
                send2[k, a] = keep[k, side, half].astype(jnp.bfloat16)
            copy2(k).start()

        @pl.when((s >= 2) & (s < STEPS + 2))
        def _():
            k = block_of(s - 2)
            copy2(k).wait_recv()
            side, half = spot(1, 0, core)
            done = keep[k, side, half] + recv2[k, 1].astype(jnp.float32)
            send3[k] = done.astype(jnp.bfloat16)
            copy3(k).start()
            keep[k, x, y] = keep[k, x, y] + recv2[k, 0].astype(jnp.float32)

        @pl.when(s >= 3)
        def _():
            k = block_of(s - 3)
            copy3(k).wait_recv()
            done = keep[k, x, y] + recv3[k].astype(jnp.float32)
            keep[k, x, y] = done

            @pl.when(s - 3 < STEPS - CHUNKS)
            def _():
                send4[k] = done.astype(jnp.bfloat16)
                copy4(k).start()

        return carry

    lax.fori_loop(0, STEPS + 3, step, 0)

    for part in range(CHUNKS):
        home = pl.ds(pl.multiple_of(r * TOK + part * PIECE, PIECE), PIECE)
        total = hid[home, cols(c, PART)].astype(jnp.float32) + keep[part, x, y]
        for d in range(1, DEPTH):
            k = d * CHUNKS + part
            copy4(k).wait_recv()
            total = total + recv4[k].astype(jnp.float32)
        out_ref[part * PIECE : (part + 1) * PIECE, :] = total.astype(jnp.bfloat16)

    sends("wait_send")
    handovers("wait_send")
    wo_sends("wait_send")
    z_sends("wait_send")

    @pl.when(outer == 0)
    def _():
        for i in range(1, 3):
            wo_relay(i)[1].wait_send()
        z_relay(1).wait_send()
        z_relay(3).wait_send()

    stream_copy(y).wait_send()
    att_copy(y).wait_send()
    for i in range(2):
        head_copy(i).wait_send()
    cross_copy().wait_send()
    for k in range(1, COLS):
        gain_copy(k, c).wait_send()
    for k in range(1, ROWS):
        w_copy(k).wait_send()
        for i in range(3):
            sh_copy(i, k, r).wait_send()
    for d in range(DEPTH):
        a_copy(d, 0).wait_send()
        for a in range(2):
            b_copy(d, a, 0).wait_send()
            for b in range(2):
                c_copy(d, a, b, core).wait_send()
    for k in range(STEPS):
        for i in range(2):
            copy1(k, i).wait_send()
        copy2(k).wait_send()
        copy3(k).wait_send()
        if k >= CHUNKS:
            copy4(k).wait_send()


def fused_body(
    queries,
    key_vectors,
    values,
    sink_logit,
    lengths,
    stream,
    out_weight,
    norm_gain,
    shared_gate,
    shared_up,
    shared_down,
    shared_switch,
    expert_gate,
    expert_up,
    expert_down,
    routes,
    route_weights,
):
    bf16, f32 = jnp.bfloat16, jnp.float32

    def sems(*shape):
        return [pltpu.SemaphoreType.DMA(shape)] * 2

    vmem = pl.BlockSpec(memory_space=pltpu.VMEM)
    hbm = pl.BlockSpec(memory_space=pltpu.HBM)
    hidden_units = expert_down.shape[1]
    return pl.pallas_call(
        layer_kernel,
        out_shape=(
            jax.ShapeDtypeStruct(queries.shape, bf16),
            jax.ShapeDtypeStruct(stream.shape, bf16),
        ),
        in_specs=[hbm] * 17,
        out_specs=(vmem, vmem),
        scratch_shapes=[
            pltpu.VMEM(queries.shape, bf16),
            pltpu.SMEM(sink_logit.shape, f32),
            pltpu.SMEM(lengths.shape, jnp.int32),
            pltpu.VMEM((PART // HDIM, HDIM), bf16),
            pltpu.VMEM((WIDTH // HDIM, HDIM), bf16),
            pltpu.VMEM(routes.T.shape, jnp.int32),
            pltpu.VMEM(route_weights.T.shape, f32),
            pltpu.VMEM((3, hidden_units + UNITS, WIDTH), bf16),
            pltpu.VMEM((8, PART), f32),
            pltpu.VMEM((8, WIDTH), f32),
            pltpu.VMEM((ROWS, 8, TOK), f32),
            pltpu.VMEM((2, (REACH + 1) * TOK, 2 * HDIM), bf16),
            pltpu.VMEM((2 * HDIM, DEPTH * SLICE), bf16),
            pltpu.VMEM((8, WIDTH), f32),
            pltpu.VMEM((ROWS, 8, TOK), f32),
            pltpu.VMEM((ROWS, TOK, TOK), f32),
            pltpu.VMEM((PLANE, 2 * HDIM), bf16),
            pltpu.VMEM((PLANE, SLICE), bf16),
            pltpu.VMEM((2, PLANE, SLICE), bf16),
            pltpu.VMEM((2, PLANE, SLICE), bf16),
            pltpu.VMEM((PLANE, SLICE), bf16),
            pltpu.VMEM((PLANE, SLICE), bf16),
            pltpu.VMEM((ROWS * TOK, WIDTH), bf16),
            pltpu.VMEM((STEPS, 2, 2, PIECE, PART), f32),
            pltpu.VMEM((STEPS, 2, 2, PIECE, PART), bf16),
            pltpu.VMEM((STEPS, 2, 2, PIECE, PART), bf16),
            pltpu.VMEM((STEPS, 2, PIECE, PART), bf16),
            pltpu.VMEM((STEPS, 2, PIECE, PART), bf16),
            pltpu.VMEM((STEPS, PIECE, PART), bf16),
            pltpu.VMEM((STEPS, PIECE, PART), bf16),
            pltpu.VMEM((STEPS, PIECE, PART), bf16),
            pltpu.VMEM((STEPS, PIECE, PART), bf16),
            pltpu.SemaphoreType.DMA((17,)),
        ]
        + sems(2, ROWS)
        + sems(2 * DEPTH)
        + sems(COLS)
        + sems(3 * ROWS)
        + sems(ROWS)
        + sems(2)
        + sems(3)
        + sems(2 * DEPTH)
        + sems(DEPTH)
        + sems(2 * DEPTH)
        + sems(4 * DEPTH)
        + sems(STEPS, 2)
        + sems(STEPS)
        + sems(STEPS)
        + sems(STEPS),
        compiler_params=pltpu.CompilerParams(
            collective_id=0, has_side_effects=True, vmem_limit_bytes=60 << 20
        ),
    )(
        queries,
        key_vectors,
        values,
        sink_logit,
        lengths,
        stream,
        out_weight,
        norm_gain.reshape(PART // HDIM, HDIM),
        shared_gate.T,
        shared_up.T,
        shared_down,
        shared_switch.reshape(WIDTH // HDIM, HDIM),
        expert_gate[0].T,
        expert_up[0].T,
        expert_down[0],
        routes.T,
        route_weights.T,
    )


def gathered_body(
    queries,
    key_vectors,
    values,
    sink_logit,
    lengths,
    stream,
    out_weight,
    norm_gain,
    shared_gate,
    shared_up,
    shared_down,
    shared_switch,
    expert_gate,
    expert_up,
    expert_down,
    routes,
    route_weights,
):
    local_tokens = queries.shape[0]
    feature_width = queries.shape[1]
    head_count = feature_width // HDIM
    my_row = lax.axis_index("row")
    positions = my_row * local_tokens + jnp.arange(local_tokens, dtype=jnp.int32)
    lower_bound = lower_bounds(lengths, positions)
    query_heads = queries.reshape(local_tokens, head_count, HDIM)
    score_scale = 1.0 / math.sqrt(HDIM)
    key_value = jnp.stack([key_vectors, values], 0)
    key_piece = lax.all_gather(key_value, "row", axis=1, tiled=True)
    row_max = jnp.broadcast_to(sink_logit[None, :], (local_tokens, head_count))
    denominator = jnp.ones((local_tokens, head_count), jnp.float32)
    numerator = jnp.zeros((local_tokens, head_count, HDIM), jnp.float32)
    needed = key_piece.shape[1]
    key_heads = key_piece[0].reshape(needed, head_count, HDIM)
    value_heads = key_piece[1].reshape(needed, head_count, HDIM)
    scores = (
        jnp.einsum("qhd,khd->qhk", query_heads, key_heads, preferred_element_type=jnp.float32)
        * score_scale
    )
    key_places = jnp.arange(needed, dtype=jnp.int32)
    visible = (
        (key_places[None, :] >= lower_bound[:, None]) & (key_places[None, :] <= positions[:, None])
    )[:, None, :]
    masked = jnp.where(visible, scores, masked_score)
    new_max = jnp.maximum(row_max, jnp.max(masked, axis=2))
    weight = jnp.where(visible, jnp.exp(masked - new_max[:, :, None]), 0.0)
    rescale = jnp.exp(row_max - new_max)
    denominator = denominator * rescale + jnp.sum(weight, axis=2)
    numerator = numerator * rescale[:, :, None] + jnp.einsum(
        "qhk,khd->qhd", weight.astype(jnp.bfloat16), value_heads, preferred_element_type=jnp.float32
    )
    final_max, denominator, numerator = (new_max, denominator, numerator)
    attended = (
        (numerator / denominator[:, :, None])
        .reshape(local_tokens, feature_width)
        .astype(jnp.bfloat16)
    )
    head_terms = jnp.dot(
        attended,
        lax.all_gather(out_weight, "row", axis=1, tiled=True),
        preferred_element_type=jnp.float32,
    )
    mixed_heads = lax.psum_scatter(
        head_terms.astype(jnp.bfloat16), "col", scatter_dimension=1, tiled=True
    ).astype(jnp.float32)
    hidden = (stream.astype(jnp.float32) + mixed_heads).astype(jnp.bfloat16)
    widened = hidden.astype(jnp.float32)
    full_width = lax.axis_size("col") * hidden.shape[1]
    squares = lax.psum(jnp.sum(widened * widened, axis=1), "col")
    row_scale = lax.rsqrt(squares / full_width + norm_eps)
    normed_part = (widened * row_scale[:, None] * norm_gain.astype(jnp.float32)).astype(
        jnp.bfloat16
    )
    normed = lax.all_gather(normed_part, "col", axis=1, tiled=True)
    gate_part = jnp.dot(
        normed,
        lax.all_gather(shared_gate, "row", axis=0, tiled=True),
        preferred_element_type=jnp.float32,
    )
    up_part = jnp.dot(
        normed,
        lax.all_gather(shared_up, "row", axis=0, tiled=True),
        preferred_element_type=jnp.float32,
    )
    shared_act = (jax.nn.silu(gate_part) * up_part).astype(jnp.bfloat16)
    shared_part = jnp.dot(
        shared_act,
        lax.all_gather(shared_down, "row", axis=1, tiled=True),
        preferred_element_type=jnp.float32,
    )
    switch = jax.nn.sigmoid(jnp.dot(normed, shared_switch, preferred_element_type=jnp.float32))
    row_count = lax.axis_size("row")
    fanout = routes.shape[1]
    model_width = normed.shape[1]
    capacity = max(2, min(local_tokens, 3 * local_tokens * fanout // (2 * row_count)))
    flat_routes = routes.reshape(-1)
    order = jnp.arange(flat_routes.shape[0])
    before = (order[None, :] < order[:, None]) & (flat_routes[None, :] == flat_routes[:, None])
    slot_index = jnp.sum(before.astype(jnp.int32), axis=1)
    target = flat_routes * capacity + slot_index
    owner_row = jnp.arange(local_tokens * fanout, dtype=jnp.int32) // fanout
    source = jnp.full((row_count * capacity,), local_tokens, jnp.int32).at[target].set(owner_row)
    padded = jnp.concatenate([normed, jnp.zeros((1, model_width), jnp.bfloat16)], 0)
    outgoing = padded[source].reshape(row_count, capacity, model_width)
    received = lax.all_to_all(outgoing, "row", split_axis=0, concat_axis=0, tiled=True)
    senders, slot_count, received_width = received.shape
    dispatched = received.reshape(senders * slot_count, received_width)
    gate_out = jnp.dot(dispatched, expert_gate[0], preferred_element_type=jnp.float32)
    up_out = jnp.dot(dispatched, expert_up[0], preferred_element_type=jnp.float32)
    activation = (jax.nn.silu(gate_out) * up_out).astype(jnp.bfloat16)
    partial_out = jnp.dot(activation, expert_down[0], preferred_element_type=jnp.float32).astype(
        jnp.bfloat16
    )
    returned = lax.all_to_all(
        partial_out.reshape(senders, slot_count, received_width),
        "row",
        split_axis=0,
        concat_axis=0,
        tiled=True,
    )
    route_rows = returned.reshape(row_count * capacity, model_width)[target].reshape(
        local_tokens, fanout, model_width
    )
    routed = jnp.zeros((local_tokens, model_width), jnp.float32)
    for route_slot in range(fanout):
        routed = routed + route_weights[:, route_slot][:, None] * route_rows[
            :, route_slot, :
        ].astype(jnp.float32)
    layer_terms = switch[:, None] * shared_part + routed
    summed = lax.psum_scatter(
        layer_terms.astype(jnp.bfloat16), "col", scatter_dimension=1, tiled=True
    ).astype(jnp.float32)
    layer_out = (hidden.astype(jnp.float32) + summed).astype(jnp.bfloat16)
    return (attended, layer_out)


def solution(mesh):
    small = mesh.shape["row"] == ROWS and mesh.shape["col"] == COLS
    return jax.shard_map(
        fused_body if small else gathered_body,
        mesh=mesh,
        in_specs=(
            P("row", "col"),
            P("row", "col"),
            P("row", "col"),
            P("col"),
            P(),
            P("row", "col"),
            P("col", "row"),
            P("col"),
            P("row", "col"),
            P("row", "col"),
            P("col", "row"),
            P(),
            P("row", None, "col"),
            P("row", None, "col"),
            P("row", "col", None),
            P("row", None),
            P("row", None),
        ),
        out_specs=(P("row", "col"), P("row", "col")),
        check_vma=False,
    )
```
